32 devices in a mesh: groups: 2 (over x), ep: 16 (over z, y, core).
Axes of the slice: x: 2, y: 2, z: 4, core: 2. Of those that a mesh axis runs over, the one named last changes fastest.
Arguments:
- resid: bfloat16 [4096, 2048], P(('groups', 'ep')), parts along dimension 0, may hold values from -12 to 12
- norm_gain: float32 [2048], replicated, may hold values from 0.1 to 1.9
- expert_ids: int32 [4096, 8], P(('groups', 'ep')), parts along dimension 0, may hold values from 0 to 15, as said below
- route_weights: float32 [4096, 8], P(('groups', 'ep')), parts along dimension 0, may hold values from 0.05 to 1
- w_in: bfloat16 [16, 2048, 1536], P('ep'), may hold values from -0.125 to 0.125
- w_out: bfloat16 [16, 768, 2048], P('ep'), may hold values from -0.21875 to 0.21875
Outputs:
- layer_out: bfloat16 [4096, 2048], P(('groups', 'ep')), parts along dimension 0
The draws below stay inside these ranges and needn't reach their ends.
There are 2 independent parts, one for each index of `groups`. The reference program is written for one: setup_inputs(seed, part) draws one part's arguments, and reference() takes and returns one part's arrays. A program takes and returns all parts, laid end to end along the dimension named above; an argument that names none is the same for every part. Nothing has to cross between parts.
Inputs may be any that keep to these rules, and one draw needn't show every extreme that they name: `expert_ids`: each row names 8 different experts. Among the rows of one device no expert is named by more than 96 rows, and in every draw one expert is named by exactly 96 rows of every device.
All inputs are finite; a program needn't handle non-finite values.
Results may differ from the reference program's by a relative error of at most 0.0053.
Values may be sent and summed in bfloat16 or wider, within the bound.
A program may use at most 128 MiB of HBM per device.

```python
import math
import jax
import jax.numpy as jnp
from jax import lax

D = 2048
TOPK = 8
FF = 768
TOK_DEV = 128
EXPERTS = 16
TOKENS = 2048
CAP = 96


def draw_resid(key, part):
    first_key, second_key, third_key = jax.random.split(key, 3)
    base = jnp.clip(jax.random.normal(first_key, (TOKENS, D), jnp.float32), -4.0, 4.0)
    row_scale = jnp.exp(jax.random.uniform(second_key, (TOKENS, 1), jnp.float32, jnp.log(0.1), jnp.log(1.0)))
    column_scale = jnp.exp(jax.random.uniform(third_key, (1, D), jnp.float32, jnp.log(0.3), jnp.log(3.0)))
    return (base * row_scale * column_scale).astype(jnp.bfloat16)


def draw_expert_ids(key, part):
    blocks = TOKENS // TOK_DEV
    slot_total = EXPERTS * CAP
    chosen_count = TOK_DEV * TOPK
    favour = jax.random.randint(jax.random.fold_in(key, 11), (EXPERTS,), 0, slot_total)
    hot_expert = jax.random.randint(jax.random.fold_in(key, 12), (), 0, EXPERTS)
    expert_of = jnp.arange(slot_total, dtype=jnp.int32) // CAP
    order_key = slot_total - 1 - jnp.arange(slot_total, dtype=jnp.int32)

    def one_block(block):
        block_key = jax.random.fold_in(key, block + 100)
        noise = jax.random.randint(jax.random.fold_in(block_key, 1), (slot_total,), 0, slot_total)
        score = noise + favour[expert_of] + jnp.where(expert_of == hot_expert, 2 * slot_total, 0)
        unused, picked = lax.top_k(score * slot_total + order_key, chosen_count)
        marked = jnp.zeros((slot_total,), jnp.int32).at[picked].set(1)
        unused_too, ordered = lax.top_k(marked * slot_total + order_key, chosen_count)
        listed = (ordered // CAP).reshape(TOPK, TOK_DEV).T
        shuffle = jax.random.permutation(jax.random.fold_in(block_key, 2), TOK_DEV)
        return listed[shuffle]
    drawn = jax.vmap(one_block)(jnp.arange(blocks, dtype=jnp.int32))
    return drawn.reshape(TOKENS, TOPK).astype(jnp.int32)


def levels(stream_key, shape, cuts, smallest, top_value):
    loudness, own = 1.0, jax.random.fold_in(stream_key, 6)
    for dim, parts in cuts:
        heights = jnp.exp(jax.random.uniform(jax.random.fold_in(own, dim), (parts,), jnp.float32, smallest / len(cuts), top_value / len(cuts)))
        loudness = loudness * jnp.repeat(heights, shape[dim] // parts).reshape([-1 if axis == dim else 1 for axis in range(len(shape))])
    return loudness


def scatter_about(own_key, shape, width, limit, cuts=(), held_as=jnp.bfloat16):
    level = levels(own_key, shape, cuts, -0.22, 0.18) if cuts else 1.0
    values = jax.random.normal(own_key, shape, jnp.float32) * width * level
    return jnp.minimum(jnp.maximum(values, -limit), limit).astype(held_as)


def setup_inputs(seed: int = 0, part: int = 0) -> dict:
    key_list = jax.random.split(jax.random.key(seed), 7)
    part_keys = jax.random.split(jax.random.fold_in(key_list[6], part), 7)
    return {
        "resid": draw_resid(jax.random.fold_in(jax.random.fold_in(key_list[6], part), 71), part),
        "norm_gain": jnp.clip(1.0 + 0.18 * jax.random.normal(key_list[1], (D,), jnp.float32), 0.1, 1.9),
        "expert_ids": draw_expert_ids(jax.random.fold_in(jax.random.fold_in(key_list[6], part), 71), part),
        "route_weights": jnp.clip(jnp.exp(math.log(1.0) - 2.9957323 * jax.random.uniform(part_keys[3], (TOKENS, TOPK), jnp.float32) ** levels(part_keys[3], (TOKENS, TOPK), ((0, 16),), -0.2, 0.2)), 0.05, 1.0),
        "w_in": scatter_about(key_list[4], (EXPERTS, D, 2 * FF), D ** -0.5, 0.125, ((0, 16),)),
        "w_out": scatter_about(key_list[5], (EXPERTS, FF, D), FF ** -0.5, 0.21875, ((0, 16),)),
    }


def apply_expert(block_rows, weight_in, weight_out):
    projected = jnp.dot(block_rows, weight_in, preferred_element_type=jnp.float32)
    gate_part = projected[:, :FF]
    up_part = projected[:, FF:]
    activated = (jax.nn.silu(gate_part) * up_part).astype(jnp.bfloat16)
    return jnp.dot(activated, weight_out, preferred_element_type=jnp.float32).astype(jnp.bfloat16)

def reference(resid, norm_gain, expert_ids, route_weights, w_in, w_out):
    token_count, model_width = resid.shape
    blocks = token_count // TOK_DEV
    resid_wide = resid.astype(jnp.float32)
    scale = lax.rsqrt(lax.optimization_barrier(jnp.mean(resid_wide * resid_wide, axis=-1, keepdims=True)) + 1e-06)
    normed = (resid_wide * scale * norm_gain).astype(jnp.bfloat16)
    mix_weights = route_weights / lax.optimization_barrier(jnp.sum(route_weights, axis=-1, keepdims=True))
    flat_ids = expert_ids.reshape(blocks, TOK_DEV * TOPK).astype(jnp.int32)
    onehot = (flat_ids[:, :, None] == jnp.arange(EXPERTS, dtype=jnp.int32)[None, None, :]).astype(jnp.int32)
    position = lax.optimization_barrier(jnp.sum((jnp.cumsum(onehot, axis=1) - onehot) * onehot, axis=-1)).astype(jnp.int32)
    column = (jnp.arange(blocks, dtype=jnp.int32)[:, None] * CAP + position).astype(jnp.int32)
    token_of = jnp.repeat(jnp.arange(token_count, dtype=jnp.int32), TOPK).reshape(blocks, TOK_DEV * TOPK)
    table = jnp.zeros((EXPERTS, blocks * CAP), jnp.int32).at[flat_ids, column].set(token_of)
    weight_table = jnp.zeros((EXPERTS, blocks * CAP), jnp.float32).at[flat_ids, column].set(mix_weights.reshape(blocks, TOK_DEV * TOPK))

    def one_expert(total, inputs):
        weight_in, weight_out, token_rows, row_weights = inputs
        outputs = apply_expert(normed[token_rows], weight_in, weight_out)
        total = total.at[token_rows].add(row_weights[:, None] * outputs.astype(jnp.float32))
        return (total, None)
    total, _ = lax.scan(one_expert, jnp.zeros((token_count, model_width), jnp.float32), (w_in, w_out, table, weight_table))
    return (resid_wide + total).astype(jnp.bfloat16)
```

```python
import functools

import jax
import jax.numpy as jnp
from jax import lax
from jax.experimental import pallas as pl
from jax.experimental.pallas import tpu as pltpu
from jax.sharding import PartitionSpec as P


PLANE = 4
MESH = pl.DeviceIdType.MESH


def flip(index, bits):
    bit = 1
    while bit <= bits:
        if bits & bit:
            index = index + bit - 2 * bit * ((index // bit) % 2)
        bit *= 2
    return index


def moe_kernel(
    count, x_ref, table_ref, resid_ref, win_hbm, wout_hbm, o_ref,
    gathered, weights, weight_cols, win, wout, hidden, partial, from_core, from_y, from_z,
    load_sem, table_send, table_recv, z_send, z_recv, y_send, y_recv, core_send, core_recv,
    fwd_send, fwd_recv, rc_send, rc_recv, ry_send, ry_recv, rz_send, rz_recv,
):
    rows, width = x_ref.shape
    units = wout.shape[0]
    planes = count // PLANE
    me = lax.axis_index("ep")
    z, q = me // PLANE, me % PLANE
    y, c = q // 2, q % 2
    core_mate = z * PLANE + flip(q, 1)
    y_mate = z * PLANE + flip(q, 2)

    def remote(src, dst, send, recv, target):
        return pltpu.make_async_remote_copy(
            src_ref=src, dst_ref=dst, send_sem=send, recv_sem=recv,
            device_id={"ep": target}, device_id_type=MESH,
        )

    load_in = pltpu.make_async_copy(win_hbm.at[0], win, load_sem.at[0])
    load_out = pltpu.make_async_copy(wout_hbm.at[0], wout, load_sem.at[1])
    load_in.start()
    load_out.start()

    barrier = pltpu.get_barrier_semaphore()
    for k in range(1, count):
        pl.semaphore_signal(
            barrier, inc=1, device_id={"ep": lax.rem(me + k, count)}, device_id_type=MESH
        )
    pl.semaphore_wait(barrier, count - 1)

    started = []

    def begin(copy):
        copy.start()
        started.append(copy)
        return copy

    plane_of = [flip(z, s) for s in range(planes)]
    to_z, to_y, to_core, to_fwd = {}, {}, {}, {}
    red_core, red_y, red_z = {}, {}, {}

    def spread(s):
        src = x_ref if s == 0 else gathered.at[plane_of[s], q]
        dst = gathered.at[plane_of[s], q]
        to_y[s] = begin(remote(src, dst, y_send.at[s], y_recv.at[s], y_mate))
        to_core[s] = begin(remote(src, dst, core_send.at[s], core_recv.at[s], core_mate))

    def forward(s):
        to_y[s].wait_recv()
        block = gathered.at[plane_of[s], flip(q, 2)]
        to_fwd[s] = begin(remote(block, block, fwd_send.at[s], fwd_recv.at[s], core_mate))

    spread(0)
    for s in range(1, planes):
        to_z[s] = begin(
            remote(
                x_ref, gathered.at[z, q], z_send.at[s], z_recv.at[s],
                plane_of[s] * PLANE + q,
            )
        )
    tables = []
    for k in range(1, count):
        target = lax.rem(me + k, count)
        tables.append(
            begin(
                remote(
                    table_ref.at[target], weights.at[me],
                    table_send.at[k - 1], table_recv.at[k - 1], target,
                )
            )
        )
    gathered[z, q] = x_ref[...]
    weights[me] = table_ref[me]
    for copy in tables:
        copy.wait_recv()

    tile_in = 256 if units % 256 == 0 else units
    tile_out = 512 if width % 512 == 0 else width

    def experts(s):
        plane = plane_of[s]
        eye = lax.broadcasted_iota(jnp.int32, (rows, rows), 0) == lax.broadcasted_iota(
            jnp.int32, (rows, rows), 1
        )
        for k in range(PLANE):
            lane = jnp.broadcast_to(weights[plane * PLANE + k], (rows, rows))
            column = jnp.sum(jnp.where(eye, lane, 0.0), axis=1, keepdims=True)
            weight_cols[pl.ds(k * rows, rows), :] = jnp.broadcast_to(column, (rows, 128))

        @pl.loop(0, units // tile_in)
        def _(j):
            gate_at = pl.multiple_of(j * tile_in, 128)
            up_at = pl.multiple_of(units + j * tile_in, 128)
            block = gathered[plane].reshape(PLANE * rows, width)
            gate = jnp.dot(
                block, win[:, pl.ds(gate_at, tile_in)], preferred_element_type=jnp.float32
            )
            up = jnp.dot(block, win[:, pl.ds(up_at, tile_in)], preferred_element_type=jnp.float32)
            act = gate / (1.0 + jnp.exp(-gate)) * up
            hidden[:, pl.ds(gate_at, tile_in)] = act.astype(jnp.bfloat16)

        @pl.loop(0, width // tile_out)
        def _(j):
            at = pl.multiple_of(j * tile_out, 128)
            made = jnp.dot(
                hidden[...], wout[:, pl.ds(at, tile_out)], preferred_element_type=jnp.float32
            )
            made = made.astype(jnp.bfloat16).astype(jnp.float32)
            for k in range(PLANE):
                cols = weight_cols[pl.ds(k * rows, rows), :]
                pieces = [
                    made[k * rows : (k + 1) * rows, i * 128 : (i + 1) * 128] * cols
                    for i in range(tile_out // 128)
                ]
                partial[s, k % 2, k // 2, :, pl.ds(at, tile_out)] = jnp.concatenate(
                    pieces, axis=1
                ).astype(jnp.bfloat16)

    def reduce_core(s):
        red_core[s] = begin(
            remote(
                partial.at[s, flip(c, 1)], from_core.at[s], rc_send.at[s], rc_recv.at[s], core_mate
            )
        )

    step = 16

    def reduce_y(s):
        red_core[s].wait_recv()

        @pl.loop(0, rows // step)
        def _(i):
            at = pl.ds(pl.multiple_of(i * step, step), step)
            for k in range(2):
                total = partial[s, c, k, at, :].astype(jnp.float32) + from_core[
                    s, k, at, :
                ].astype(jnp.float32)
                partial[s, c, k, at, :] = total.astype(jnp.bfloat16)

        red_y[s] = begin(
            remote(
                partial.at[s, c, flip(y, 1)], from_y.at[s], ry_send.at[s], ry_recv.at[s], y_mate
            )
        )

    def reduce_z(s):
        red_y[s].wait_recv()

        @pl.loop(0, rows // step)
        def _(i):
            at = pl.ds(pl.multiple_of(i * step, step), step)
            total = partial[s, c, y, at, :].astype(jnp.float32) + from_y[s, at, :].astype(
                jnp.float32
            )
            partial[s, c, y, at, :] = total.astype(jnp.bfloat16)

        if s:
            red_z[s] = begin(
                remote(
                    partial.at[s, c, y], from_z.at[s - 1], rz_send.at[s], rz_recv.at[s],
                    plane_of[s] * PLANE + q,
                )
            )

    def arrive(s):
        if s < planes:
            to_z[s].wait_recv()
            spread(s)

    forward(0)
    arrive(1)
    load_in.wait()
    load_out.wait()
    for s in range(planes):
        to_core[s].wait_recv()
        to_fwd[s].wait_recv()
        experts(s)
        reduce_core(s)
        arrive(s + 2)
        if s + 1 < planes:
            forward(s + 1)
        reduce_y(s)
        if s:
            reduce_z(s - 1)
    reduce_z(planes - 1)
    for s in range(1, planes):
        red_z[s].wait_recv()

    @pl.loop(0, rows // step)
    def _(i):
        at = pl.ds(pl.multiple_of(i * step, step), step)
        total = partial[0, c, y, at, :].astype(jnp.float32)
        for s in range(1, planes):
            total = total + from_z[s - 1, at, :].astype(jnp.float32)
        o_ref[at, :] = (resid_ref[at, :].astype(jnp.float32) + total).astype(jnp.bfloat16)

    for copy in started:
        copy.wait_send()


def vmem_bytes(count, rows, width, units):
    block = 2 * rows * width
    return (
        block * (4 * 2 * (count // PLANE) + 8) + 2 * 3 * units * width
        + 2 * PLANE * rows * units + 8 * count * rows * 4
    )


def local(resid, norm_gain, expert_ids, route_weights, w_in, w_out):
    rows, width = resid.shape
    units = w_out.shape[1]
    count = lax.axis_size("ep")
    planes = count // PLANE
    fits = vmem_bytes(count, rows, width, units) <= 44 * 2**20
    if count % PLANE or planes < 2 or planes & (planes - 1) or rows != 128 or not fits:
        return local_wide(resid, norm_gain, expert_ids, route_weights, w_in, w_out)
    resid_wide = resid.astype(jnp.float32)
    scale = lax.rsqrt(jnp.mean(resid_wide * resid_wide, axis=-1, keepdims=True) + 1e-06)
    normed = (resid_wide * scale * norm_gain).astype(jnp.bfloat16)
    mix_weights = route_weights / jnp.sum(route_weights, axis=-1, keepdims=True)
    experts = jnp.arange(count, dtype=jnp.int32)[:, None, None]
    table = jnp.sum(jnp.where(expert_ids[None] == experts, mix_weights[None], 0.0), axis=-1)
    table = table.reshape(count, 1, rows)
    vmem = pl.BlockSpec(memory_space=pltpu.VMEM)
    hbm = pl.BlockSpec(memory_space=pl.ANY)
    bf16 = jnp.bfloat16
    dma = pltpu.SemaphoreType.DMA
    return pl.pallas_call(
        functools.partial(moe_kernel, count),
        out_shape=jax.ShapeDtypeStruct((rows, width), bf16),
        in_specs=[vmem, vmem, vmem, hbm, hbm],
        out_specs=vmem,
        scratch_shapes=[
            pltpu.VMEM((planes, PLANE, rows, width), bf16),
            pltpu.VMEM((count, 1, rows), jnp.float32),
            pltpu.VMEM((PLANE * rows, 128), jnp.float32),
            pltpu.VMEM((width, 2 * units), bf16),
            pltpu.VMEM((units, width), bf16),
            pltpu.VMEM((PLANE * rows, units), bf16),
            pltpu.VMEM((planes, 2, 2, rows, width), bf16),
            pltpu.VMEM((planes, 2, rows, width), bf16),
            pltpu.VMEM((planes, rows, width), bf16),
            pltpu.VMEM((planes - 1, rows, width), bf16),
            dma((2,)),
            dma((count - 1,)),
            dma((count - 1,)),
        ]
        + [dma((planes,))] * 14,
        compiler_params=pltpu.CompilerParams(
            collective_id=0, has_side_effects=True, vmem_limit_bytes=60 * 2**20
        ),
    )(normed, table, resid, w_in, w_out)


def local_wide(resid, norm_gain, expert_ids, route_weights, w_in, w_out):
    token_rows, model_width = resid.shape
    top_count = expert_ids.shape[1]
    ep_devices = lax.axis_size("ep")
    capacity = 3 * token_rows * top_count // (2 * ep_devices)
    weight_in = w_in[0]
    weight_out = w_out[0]
    hidden_units = weight_out.shape[0]
    resid_wide = resid.astype(jnp.float32)
    scale = lax.rsqrt(jnp.mean(resid_wide * resid_wide, axis=-1, keepdims=True) + 1e-06)
    normed = (resid_wide * scale * norm_gain).astype(jnp.bfloat16)
    mix_weights = route_weights / jnp.sum(route_weights, axis=-1, keepdims=True)
    flat_ids = expert_ids.reshape(-1)
    onehot = (flat_ids[:, None] == jnp.arange(ep_devices, dtype=jnp.int32)[None, :]).astype(
        jnp.int32
    )
    position = jnp.sum((jnp.cumsum(onehot, axis=0) - onehot) * onehot, axis=1)
    slot_index = flat_ids * capacity + position
    all_normed, all_ids = (
        lax.all_gather(normed, "ep", axis=0, tiled=True),
        lax.all_gather(expert_ids, "ep", axis=0, tiled=True),
    )
    own_expert = lax.axis_index("ep")
    row_hits = (
        jnp.any(all_ids == own_expert, axis=1).astype(jnp.int32).reshape(ep_devices, token_rows)
    )
    placing = jnp.cumsum(row_hits, axis=1) - row_hits
    target = jnp.where(
        row_hits == 1,
        jnp.arange(ep_devices, dtype=jnp.int32)[:, None] * capacity + placing,
        ep_devices * capacity,
    ).reshape(-1)
    received = (
        jnp.zeros((ep_devices * capacity, model_width), jnp.bfloat16)
        .at[target]
        .set(all_normed, mode="drop")
    )
    block_rows = received.reshape(ep_devices, capacity, model_width)
    rows_flat = block_rows.reshape(-1, model_width)
    projected = jnp.dot(rows_flat, weight_in, preferred_element_type=jnp.float32)
    activated = (jax.nn.silu(projected[:, :hidden_units]) * projected[:, hidden_units:]).astype(
        jnp.bfloat16
    )
    produced = jnp.dot(activated, weight_out, preferred_element_type=jnp.float32).astype(
        jnp.bfloat16
    )
    outputs = produced.reshape(block_rows.shape)
    returned = lax.all_to_all(outputs, "ep", split_axis=0, concat_axis=0, tiled=True).reshape(
        -1, model_width
    )
    picked = returned[slot_index].reshape(token_rows, top_count, model_width).astype(jnp.float32)
    mixed = jnp.sum(mix_weights[:, :, None] * picked, axis=1)
    return (resid_wide + mixed).astype(jnp.bfloat16)


def solution(mesh):
    in_specs = (
        P(("groups", "ep"), None),
        P(),
        P(("groups", "ep"), None),
        P(("groups", "ep"), None),
        P("ep", None, None),
        P("ep", None, None),
    )
    out_specs = P(("groups", "ep"), None)
    return jax.shard_map(local, mesh=mesh, in_specs=in_specs, out_specs=out_specs, check_vma=False)
```

```python
import functools

import jax
import jax.numpy as jnp
from jax import lax
from jax.experimental import pallas as pl
from jax.experimental.pallas import tpu as pltpu
from jax.sharding import PartitionSpec as P


PLANE = 4
MESH = pl.DeviceIdType.MESH


def flip(index, bits):
    bit = 1
    while bit <= bits:
        if bits & bit:
            index = index + bit - 2 * bit * ((index // bit) % 2)
        bit *= 2
    return index


def moe_kernel(
    count, x_ref, table_ref, resid_ref, win_hbm, wout_hbm, o_ref,
    gathered, weights, weight_cols, win, wout, hidden, partial, from_core, from_y, from_z,
    load_sem, table_send, table_recv, z_send, z_recv, y_send, y_recv, core_send, core_recv,
    fwd_send, fwd_recv, rc_send, rc_recv, ry_send, ry_recv, rz_send, rz_recv,
):
    rows, width = x_ref.shape
    units = wout.shape[0]
    planes = count // PLANE
    me = lax.axis_index("ep")
    z, q = me // PLANE, me % PLANE
    y, c = q // 2, q % 2
    core_mate = z * PLANE + flip(q, 1)
    y_mate = z * PLANE + flip(q, 2)

    def remote(src, dst, send, recv, target):
        return pltpu.make_async_remote_copy(
            src_ref=src, dst_ref=dst, send_sem=send, recv_sem=recv,
            device_id={"ep": target}, device_id_type=MESH,
        )

    load_in = pltpu.make_async_copy(win_hbm.at[0], win, load_sem.at[0])
    load_out = pltpu.make_async_copy(wout_hbm.at[0], wout, load_sem.at[1])
    load_in.start()
    load_out.start()

    barrier = pltpu.get_barrier_semaphore()
    for k in range(1, count):
        pl.semaphore_signal(
            barrier, inc=1, device_id={"ep": lax.rem(me + k, count)}, device_id_type=MESH
        )
    pl.semaphore_wait(barrier, count - 1)

    started = []

    def begin(copy):
        copy.start()
        started.append(copy)
        return copy

    low, high = z, planes - 1 - z
    near = jnp.minimum(low, high)
    side = jnp.where(low < high, -1, 1)

    def visit(k):
        if k == 0:
            return z
        paired = (side if k % 2 else -side) * ((k + 1) // 2)
        return z + jnp.where(k <= 2 * near, paired, -side * (k - near))

    plane_of = [visit(k) for k in range(planes)]
    to_y, to_core, to_fwd = {}, {}, {}
    red_core, red_y, red_z = {}, {}, {}
    guarded = []

    def begin_if(condition, copy):
        @pl.when(condition)
        def _():
            copy.start()

        guarded.append((condition, copy))

    def spread(s):
        p = plane_of[s]
        src = x_ref if s == 0 else gathered.at[p, q]
        dst = gathered.at[p, q]
        to_y[s] = begin(remote(src, dst, y_send.at[s], y_recv.at[s], y_mate))
        to_core[s] = begin(remote(src, dst, core_send.at[s], core_recv.at[s], core_mate))

    def forward(s):
        to_y[s].wait_recv()
        block = gathered.at[plane_of[s], flip(q, 2)]
        to_fwd[s] = begin(remote(block, block, fwd_send.at[s], fwd_recv.at[s], core_mate))

    def z_copy(p, src, send, target_plane):
        return remote(
            src, gathered.at[p, q], z_send.at[send], z_recv.at[p], target_plane * PLANE + q
        )

    spread(0)
    begin_if(z > 0, z_copy(z, x_ref, 0, jnp.maximum(z - 1, 0)))
    begin_if(z < planes - 1, z_copy(z, x_ref, planes, jnp.minimum(z + 1, planes - 1)))
    tables = []
    for k in range(1, count):
        target = lax.rem(me + k, count)
        tables.append(
            begin(
                remote(
                    table_ref.at[target], weights.at[me],
                    table_send.at[k - 1], table_recv.at[k - 1], target,
                )
            )
        )
    gathered[z, q] = x_ref[...]
    weights[me] = table_ref[me]

    def arrive(s):
        if s >= planes:
            return
        p = plane_of[s]
        block = gathered.at[p, q]
        z_copy(p, block, s, p).wait_recv()
        onward = jnp.where(p < z, z + 1, z - 1)
        inside = jnp.logical_and(onward >= 0, onward < planes)
        begin_if(inside, z_copy(p, block, s, jnp.clip(onward, 0, planes - 1)))
        spread(s)

    tile_in = 256 if units % 256 == 0 else units
    tile_out = 512 if width % 512 == 0 else width

    def experts(s):
        plane = plane_of[s]
        eye = lax.broadcasted_iota(jnp.int32, (rows, rows), 0) == lax.broadcasted_iota(
            jnp.int32, (rows, rows), 1
        )
        for k in range(PLANE):
            lane = jnp.broadcast_to(weights[plane * PLANE + k], (rows, rows))
            column = jnp.sum(jnp.where(eye, lane, 0.0), axis=1, keepdims=True)
            weight_cols[pl.ds(k * rows, rows), :] = jnp.broadcast_to(column, (rows, 128))

        @pl.loop(0, units // tile_in)
        def _(j):
            gate_at = pl.multiple_of(j * tile_in, 128)
            up_at = pl.multiple_of(units + j * tile_in, 128)
            block = gathered[plane].reshape(PLANE * rows, width)
            gate = jnp.dot(
                block, win[:, pl.ds(gate_at, tile_in)], preferred_element_type=jnp.float32
            )
            up = jnp.dot(block, win[:, pl.ds(up_at, tile_in)], preferred_element_type=jnp.float32)
            act = gate / (1.0 + jnp.exp(-gate)) * up
            hidden[:, pl.ds(gate_at, tile_in)] = act.astype(jnp.bfloat16)

        @pl.loop(0, width // tile_out)
        def _(j):
            at = pl.multiple_of(j * tile_out, 128)
            made = jnp.dot(
                hidden[...], wout[:, pl.ds(at, tile_out)], preferred_element_type=jnp.float32
            )
            made = made.astype(jnp.bfloat16).astype(jnp.float32)
            for k in range(PLANE):
                cols = weight_cols[pl.ds(k * rows, rows), :]
                pieces = [
                    made[k * rows : (k + 1) * rows, i * 128 : (i + 1) * 128] * cols
                    for i in range(tile_out // 128)
                ]
                partial[s, k % 2, k // 2, :, pl.ds(at, tile_out)] = jnp.concatenate(
                    pieces, axis=1
                ).astype(jnp.bfloat16)

    def reduce_core(s):
        red_core[s] = begin(
            remote(
                partial.at[s, flip(c, 1)], from_core.at[s], rc_send.at[s], rc_recv.at[s], core_mate
            )
        )

    step = 16

    def reduce_y(s):
        red_core[s].wait_recv()

        @pl.loop(0, rows // step)
        def _(i):
            at = pl.ds(pl.multiple_of(i * step, step), step)
            for k in range(2):
                total = partial[s, c, k, at, :].astype(jnp.float32) + from_core[
                    s, k, at, :
                ].astype(jnp.float32)
                partial[s, c, k, at, :] = total.astype(jnp.bfloat16)

        red_y[s] = begin(
            remote(
                partial.at[s, c, flip(y, 1)], from_y.at[s], ry_send.at[s], ry_recv.at[s], y_mate
            )
        )

    def reduce_z(s):
        red_y[s].wait_recv()

        @pl.loop(0, rows // step)
        def _(i):
            at = pl.ds(pl.multiple_of(i * step, step), step)
            total = partial[s, c, y, at, :].astype(jnp.float32) + from_y[s, at, :].astype(
                jnp.float32
            )
            partial[s, c, y, at, :] = total.astype(jnp.bfloat16)

        if s:
            red_z[s] = begin(
                remote(
                    partial.at[s, c, y], from_z.at[z], rz_send.at[s], rz_recv.at[z],
                    plane_of[s] * PLANE + q,
                )
            )

    arrive(1)
    forward(0)
    load_in.wait()
    load_out.wait()
    for copy in tables:
        copy.wait_recv()
    for s in range(planes):
        to_core[s].wait_recv()
        to_fwd[s].wait_recv()
        experts(s)
        reduce_core(s)
        arrive(s + 2)
        if s + 1 < planes:
            forward(s + 1)
        if s:
            reduce_y(s)
        if s > 1:
            reduce_z(s - 1)
    reduce_y(0)
    reduce_z(planes - 1)
    reduce_z(0)
    for s in range(1, planes):
        p = plane_of[s]
        remote(
            partial.at[0, c, y], from_z.at[p], rz_send.at[s], rz_recv.at[p], p * PLANE + q
        ).wait_recv()

    @pl.loop(0, rows // step)
    def _(i):
        at = pl.ds(pl.multiple_of(i * step, step), step)
        total = partial[0, c, y, at, :].astype(jnp.float32)
        for s in range(1, planes):
            total = total + from_z[plane_of[s], at, :].astype(jnp.float32)
        o_ref[at, :] = (resid_ref[at, :].astype(jnp.float32) + total).astype(jnp.bfloat16)

    for copy in started:
        copy.wait_send()
    for condition, copy in guarded:

        @pl.when(condition)
        def _(copy=copy):
            copy.wait_send()


def vmem_bytes(count, rows, width, units):
    block = 2 * rows * width
    return (
        block * (4 * 2 * (count // PLANE) + 8) + 2 * 3 * units * width
        + 2 * PLANE * rows * units + 8 * count * rows * 4
    )


def local(resid, norm_gain, expert_ids, route_weights, w_in, w_out):
    rows, width = resid.shape
    units = w_out.shape[1]
    count = lax.axis_size("ep")
    planes = count // PLANE
    fits = vmem_bytes(count, rows, width, units) <= 44 * 2**20
    if count % PLANE or planes < 2 or planes & (planes - 1) or rows != 128 or not fits:
        return local_wide(resid, norm_gain, expert_ids, route_weights, w_in, w_out)
    resid_wide = resid.astype(jnp.float32)
    scale = lax.rsqrt(jnp.mean(resid_wide * resid_wide, axis=-1, keepdims=True) + 1e-06)
    normed = (resid_wide * scale * norm_gain).astype(jnp.bfloat16)
    mix_weights = route_weights / jnp.sum(route_weights, axis=-1, keepdims=True)
    experts = jnp.arange(count, dtype=jnp.int32)[:, None, None]
    table = jnp.sum(jnp.where(expert_ids[None] == experts, mix_weights[None], 0.0), axis=-1)
    table = table.reshape(count, 1, rows)
    vmem = pl.BlockSpec(memory_space=pltpu.VMEM)
    hbm = pl.BlockSpec(memory_space=pl.ANY)
    bf16 = jnp.bfloat16
    dma = pltpu.SemaphoreType.DMA
    return pl.pallas_call(
        functools.partial(moe_kernel, count),
        out_shape=jax.ShapeDtypeStruct((rows, width), bf16),
        in_specs=[vmem, vmem, vmem, hbm, hbm],
        out_specs=vmem,
        scratch_shapes=[
            pltpu.VMEM((planes, PLANE, rows, width), bf16),
            pltpu.VMEM((count, 1, rows), jnp.float32),
            pltpu.VMEM((PLANE * rows, 128), jnp.float32),
            pltpu.VMEM((width, 2 * units), bf16),
            pltpu.VMEM((units, width), bf16),
            pltpu.VMEM((PLANE * rows, units), bf16),
            pltpu.VMEM((planes, 2, 2, rows, width), bf16),
            pltpu.VMEM((planes, 2, rows, width), bf16),
            pltpu.VMEM((planes, rows, width), bf16),
            pltpu.VMEM((planes, rows, width), bf16),
            dma((2,)),
            dma((count - 1,)),
            dma((count - 1,)),
        ]
        + [dma((planes + 1,))] * 14,
        compiler_params=pltpu.CompilerParams(
            collective_id=0, has_side_effects=True, vmem_limit_bytes=60 * 2**20
        ),
    )(normed, table, resid, w_in, w_out)


def local_wide(resid, norm_gain, expert_ids, route_weights, w_in, w_out):
    token_rows, model_width = resid.shape
    top_count = expert_ids.shape[1]
    ep_devices = lax.axis_size("ep")
    capacity = 3 * token_rows * top_count // (2 * ep_devices)
    weight_in = w_in[0]
    weight_out = w_out[0]
    hidden_units = weight_out.shape[0]
    resid_wide = resid.astype(jnp.float32)
    scale = lax.rsqrt(jnp.mean(resid_wide * resid_wide, axis=-1, keepdims=True) + 1e-06)
    normed = (resid_wide * scale * norm_gain).astype(jnp.bfloat16)
    mix_weights = route_weights / jnp.sum(route_weights, axis=-1, keepdims=True)
    flat_ids = expert_ids.reshape(-1)
    onehot = (flat_ids[:, None] == jnp.arange(ep_devices, dtype=jnp.int32)[None, :]).astype(
        jnp.int32
    )
    position = jnp.sum((jnp.cumsum(onehot, axis=0) - onehot) * onehot, axis=1)
    slot_index = flat_ids * capacity + position
    all_normed, all_ids = (
        lax.all_gather(normed, "ep", axis=0, tiled=True),
        lax.all_gather(expert_ids, "ep", axis=0, tiled=True),
    )
    own_expert = lax.axis_index("ep")
    row_hits = (
        jnp.any(all_ids == own_expert, axis=1).astype(jnp.int32).reshape(ep_devices, token_rows)
    )
    placing = jnp.cumsum(row_hits, axis=1) - row_hits
    target = jnp.where(
        row_hits == 1,
        jnp.arange(ep_devices, dtype=jnp.int32)[:, None] * capacity + placing,
        ep_devices * capacity,
    ).reshape(-1)
    received = (
        jnp.zeros((ep_devices * capacity, model_width), jnp.bfloat16)
        .at[target]
        .set(all_normed, mode="drop")
    )
    block_rows = received.reshape(ep_devices, capacity, model_width)
    rows_flat = block_rows.reshape(-1, model_width)
    projected = jnp.dot(rows_flat, weight_in, preferred_element_type=jnp.float32)
    activated = (jax.nn.silu(projected[:, :hidden_units]) * projected[:, hidden_units:]).astype(
        jnp.bfloat16
    )
    produced = jnp.dot(activated, weight_out, preferred_element_type=jnp.float32).astype(
        jnp.bfloat16
    )
    outputs = produced.reshape(block_rows.shape)
    returned = lax.all_to_all(outputs, "ep", split_axis=0, concat_axis=0, tiled=True).reshape(
        -1, model_width
    )
    picked = returned[slot_index].reshape(token_rows, top_count, model_width).astype(jnp.float32)
    mixed = jnp.sum(mix_weights[:, :, None] * picked, axis=1)
    return (resid_wide + mixed).astype(jnp.bfloat16)


def solution(mesh):
    in_specs = (
        P(("groups", "ep"), None),
        P(),
        P(("groups", "ep"), None),
        P(("groups", "ep"), None),
        P("ep", None, None),
        P("ep", None, None),
    )
    out_specs = P(("groups", "ep"), None)
    return jax.shard_map(local, mesh=mesh, in_specs=in_specs, out_specs=out_specs, check_vma=False)
```

```python
import functools

import jax
import jax.numpy as jnp
from jax import lax
from jax.experimental import pallas as pl
from jax.experimental.pallas import tpu as pltpu
from jax.sharding import PartitionSpec as P


PLANE = 4
MESH = pl.DeviceIdType.MESH


def flip(index, bits):
    bit = 1
    while bit <= bits:
        if bits & bit:
            index = index + bit - 2 * bit * ((index // bit) % 2)
        bit *= 2
    return index


def moe_kernel(
    count, resid_ref, gain_ref, ids_ref, route_ref, win_hbm, wout_hbm, o_ref,
    gathered, table_ref, weights, weight_cols, win, wout, hidden, partial, from_core, from_y,
    from_z, from_near,
    load_sem, table_send, table_recv, z_send, z_recv, y_send, y_recv, core_send, core_recv,
    fwd_send, fwd_recv, rc_send, rc_recv, ry_send, ry_recv, rz_send, rz_recv, rn_send, rn_recv,
):
    rows, width = resid_ref.shape
    units = wout.shape[0]
    planes = count // PLANE
    me = lax.axis_index("ep")
    z, q = me // PLANE, me % PLANE
    y, c = q // 2, q % 2
    core_mate = z * PLANE + flip(q, 1)
    y_mate = z * PLANE + flip(q, 2)

    def remote(src, dst, send, recv, target):
        return pltpu.make_async_remote_copy(
            src_ref=src, dst_ref=dst, send_sem=send, recv_sem=recv,
            device_id={"ep": target}, device_id_type=MESH,
        )

    load_in = pltpu.make_async_copy(win_hbm.at[0], win, load_sem.at[0])
    load_out = pltpu.make_async_copy(wout_hbm.at[0], wout, load_sem.at[1])
    load_in.start()
    load_out.start()

    barrier = pltpu.get_barrier_semaphore()
    for k in range(1, count):
        pl.semaphore_signal(
            barrier, inc=1, device_id={"ep": lax.rem(me + k, count)}, device_id_type=MESH
        )

    step = 16

    @pl.loop(0, rows // step)
    def _(i):
        at = pl.ds(pl.multiple_of(i * step, step), step)
        wide = resid_ref[at, :].astype(jnp.float32)
        scale = lax.rsqrt(jnp.mean(wide * wide, axis=-1, keepdims=True) + 1e-06)
        gathered[z, q, at, :] = (wide * scale * gain_ref[...]).astype(jnp.bfloat16)

    mix = route_ref[...] / jnp.sum(route_ref[...], axis=0, keepdims=True)
    for e in range(count):
        table_ref[e] = jnp.sum(jnp.where(ids_ref[...] == e, mix, 0.0), axis=0, keepdims=True)
    weights[me] = jnp.sum(jnp.where(ids_ref[...] == me, mix, 0.0), axis=0, keepdims=True)
    pl.semaphore_wait(barrier, count - 1)

    started = []

    def begin(copy):
        copy.start()
        started.append(copy)
        return copy

    low, high = z, planes - 1 - z
    near = jnp.minimum(low, high)
    side = jnp.where(low < high, -1, 1)

    def visit(k):
        if k == 0:
            return z
        paired = (side if k % 2 else -side) * ((k + 1) // 2)
        return z + jnp.where(k <= 2 * near, paired, -side * (k - near))

    plane_of = [visit(k) for k in range(planes)]
    is_near = [False, True, near >= 1] + [False] * planes

    def when(condition, run):
        if condition is True:
            run()
        elif condition is not False:
            pl.when(condition)(run)

    def negate(condition):
        return not condition if isinstance(condition, bool) else jnp.logical_not(condition)

    to_y, to_core, to_fwd = {}, {}, {}
    red_core, red_y, red_z = {}, {}, {}
    guarded = []

    def begin_if(condition, copy):
        @pl.when(condition)
        def _():
            copy.start()

        guarded.append((condition, copy))

    def spread(s):
        p = plane_of[s]
        src = dst = gathered.at[p, q]
        to_y[s] = begin(remote(src, dst, y_send.at[s], y_recv.at[s], y_mate))
        to_core[s] = begin(remote(src, dst, core_send.at[s], core_recv.at[s], core_mate))

    def forward(s):
        to_y[s].wait_recv()
        block = gathered.at[plane_of[s], flip(q, 2)]
        to_fwd[s] = begin(remote(block, block, fwd_send.at[s], fwd_recv.at[s], core_mate))

    def z_copy(p, src, send, target_plane):
        return remote(
            src, gathered.at[p, q], z_send.at[send], z_recv.at[p], target_plane * PLANE + q
        )

    spread(0)
    begin_if(z > 0, z_copy(z, gathered.at[z, q], 0, jnp.maximum(z - 1, 0)))
    begin_if(z < planes - 1, z_copy(z, gathered.at[z, q], planes, jnp.minimum(z + 1, planes - 1)))
    tables = []
    for k in range(1, count):
        target = lax.rem(me + k, count)
        tables.append(
            begin(
                remote(
                    table_ref.at[target], weights.at[me],
                    table_send.at[k - 1], table_recv.at[k - 1], target,
                )
            )
        )
    for slot, there in ((0, z > 0), (1, z < planes - 1)):

        @pl.when(jnp.logical_not(there))
        def _(slot=slot):
            from_near[slot] = jnp.zeros(from_near.shape[1:], jnp.bfloat16)

    if planes > 2:

        @pl.when(is_near[2])
        def _():
            from_z[plane_of[2]] = jnp.zeros(from_z.shape[1:], jnp.bfloat16)

    def arrive(s):
        if s >= planes:
            return
        p = plane_of[s]
        block = gathered.at[p, q]
        z_copy(p, block, s, p).wait_recv()
        onward = jnp.where(p < z, z + 1, z - 1)
        inside = jnp.logical_and(onward >= 0, onward < planes)
        begin_if(inside, z_copy(p, block, s, jnp.clip(onward, 0, planes - 1)))
        spread(s)

    tile_in = 256 if units % 256 == 0 else units
    tile_out = 512 if width % 512 == 0 else width

    def experts(s):
        plane = plane_of[s]
        eye = lax.broadcasted_iota(jnp.int32, (rows, rows), 0) == lax.broadcasted_iota(
            jnp.int32, (rows, rows), 1
        )
        for k in range(PLANE):
            lane = jnp.broadcast_to(weights[plane * PLANE + k], (rows, rows))
            column = jnp.sum(jnp.where(eye, lane, 0.0), axis=1, keepdims=True)
            weight_cols[pl.ds(k * rows, rows), :] = jnp.broadcast_to(column, (rows, 128))

        @pl.loop(0, units // tile_in)
        def _(j):
            gate_at = pl.multiple_of(j * tile_in, 128)
            up_at = pl.multiple_of(units + j * tile_in, 128)
            block = gathered[plane].reshape(PLANE * rows, width)
            gate = jnp.dot(
                block, win[:, pl.ds(gate_at, tile_in)], preferred_element_type=jnp.float32
            )
            up = jnp.dot(block, win[:, pl.ds(up_at, tile_in)], preferred_element_type=jnp.float32)
            act = gate / (1.0 + jnp.exp(-gate)) * up
            hidden[:, pl.ds(gate_at, tile_in)] = act.astype(jnp.bfloat16)

        @pl.loop(0, width // tile_out)
        def _(j):
            at = pl.multiple_of(j * tile_out, 128)
            made = jnp.dot(
                hidden[...], wout[:, pl.ds(at, tile_out)], preferred_element_type=jnp.float32
            )
            made = made.astype(jnp.bfloat16).astype(jnp.float32)
            for k in range(PLANE):
                cols = weight_cols[pl.ds(k * rows, rows), :]
                pieces = [
                    made[k * rows : (k + 1) * rows, i * 128 : (i + 1) * 128] * cols
                    for i in range(tile_out // 128)
                ]
                partial[s, k % 2, k // 2, :, pl.ds(at, tile_out)] = jnp.concatenate(
                    pieces, axis=1
                ).astype(jnp.bfloat16)

    def reduce_core(s):
        red_core[s] = begin(
            remote(
                partial.at[s, flip(c, 1)], from_core.at[s], rc_send.at[s], rc_recv.at[s], core_mate
            )
        )

    def y_copy(s):
        return remote(
            partial.at[s, c, flip(y, 1)], from_y.at[s], ry_send.at[s], ry_recv.at[s], y_mate
        )

    def far_copy(s, source):
        return remote(
            partial.at[s, c, y], from_z.at[source], rz_send.at[s], rz_recv.at[source],
            plane_of[s] * PLANE + q,
        )

    def near_copy(s, slot):
        return remote(
            partial.at[s, c], from_near.at[slot], rn_send.at[s], rn_recv.at[slot],
            plane_of[s] * PLANE + q,
        )

    def reduce_y(s):
        red_core[s].wait_recv()
        if s == 0:
            for slot, there in ((0, z > 0), (1, z < planes - 1)):

                @pl.when(there)
                def _(slot=slot):
                    near_copy(0, slot).wait_recv()

        @pl.loop(0, rows // step)
        def _(i):
            at = pl.ds(pl.multiple_of(i * step, step), step)
            for k in range(2):
                total = partial[s, c, k, at, :].astype(jnp.float32) + from_core[
                    s, k, at, :
                ].astype(jnp.float32)
                if s == 0:
                    for slot in range(2):
                        total = total + from_near[slot, k, at, :].astype(jnp.float32)
                partial[s, c, k, at, :] = total.astype(jnp.bfloat16)

        when(is_near[s], lambda: near_copy(s, jnp.where(plane_of[s] > z, 0, 1)).start())
        when(negate(is_near[s]), lambda: y_copy(s).start())

    def reduce_z(s):
        def run():
            y_copy(s).wait_recv()

            @pl.loop(0, rows // step)
            def _(i):
                at = pl.ds(pl.multiple_of(i * step, step), step)
                total = partial[s, c, y, at, :].astype(jnp.float32) + from_y[s, at, :].astype(
                    jnp.float32
                )
                partial[s, c, y, at, :] = total.astype(jnp.bfloat16)

            far_copy(s, z).start()

        when(negate(is_near[s]), run)

    arrive(1)
    forward(0)
    load_in.wait()
    load_out.wait()
    for copy in tables:
        copy.wait_recv()
    for s in range(planes):
        to_core[s].wait_recv()
        to_fwd[s].wait_recv()
        experts(s)
        reduce_core(s)
        arrive(s + 2)
        if s + 1 < planes:
            forward(s + 1)
        if s:
            reduce_y(s)
        if s > 1:
            reduce_z(s - 1)
    if planes > 2:
        reduce_z(planes - 1)
    reduce_y(0)
    y_copy(0).wait_recv()
    for s in range(1, planes):
        when(negate(is_near[s]), lambda s=s: far_copy(s, plane_of[s]).wait_recv())

    @pl.loop(0, rows // step)
    def _(i):
        at = pl.ds(pl.multiple_of(i * step, step), step)
        total = partial[0, c, y, at, :].astype(jnp.float32) + from_y[0, at, :].astype(jnp.float32)
        for s in range(2, planes):
            total = total + from_z[plane_of[s], at, :].astype(jnp.float32)
        o_ref[at, :] = (resid_ref[at, :].astype(jnp.float32) + total).astype(jnp.bfloat16)

    for copy in started:
        copy.wait_send()
    for condition, copy in guarded:

        @pl.when(condition)
        def _(copy=copy):
            copy.wait_send()

    y_copy(0).wait_send()
    for s in range(1, planes):
        when(is_near[s], lambda s=s: near_copy(s, 0).wait_send())

        def sent(s=s):
            y_copy(s).wait_send()
            far_copy(s, z).wait_send()

        when(negate(is_near[s]), sent)


def vmem_bytes(count, rows, width, units):
    block = 2 * rows * width
    return (
        block * (4 * 2 * (count // PLANE) + 8) + 2 * 3 * units * width
        + 2 * PLANE * rows * units + 8 * count * rows * 4
    )


def local(resid, norm_gain, expert_ids, route_weights, w_in, w_out):
    rows, width = resid.shape
    units = w_out.shape[1]
    count = lax.axis_size("ep")
    planes = count // PLANE
    fits = vmem_bytes(count, rows, width, units) <= 44 * 2**20
    if count % PLANE or planes < 2 or planes & (planes - 1) or rows != 128 or not fits:
        return local_wide(resid, norm_gain, expert_ids, route_weights, w_in, w_out)
    vmem = pl.BlockSpec(memory_space=pltpu.VMEM)
    hbm = pl.BlockSpec(memory_space=pl.ANY)
    bf16 = jnp.bfloat16
    dma = pltpu.SemaphoreType.DMA
    return pl.pallas_call(
        functools.partial(moe_kernel, count),
        out_shape=jax.ShapeDtypeStruct((rows, width), bf16),
        in_specs=[vmem, vmem, vmem, vmem, hbm, hbm],
        out_specs=vmem,
        scratch_shapes=[
            pltpu.VMEM((planes, PLANE, rows, width), bf16),
            pltpu.VMEM((count, 1, rows), jnp.float32),
            pltpu.VMEM((count, 1, rows), jnp.float32),
            pltpu.VMEM((PLANE * rows, 128), jnp.float32),
            pltpu.VMEM((width, 2 * units), bf16),
            pltpu.VMEM((units, width), bf16),
            pltpu.VMEM((PLANE * rows, units), bf16),
            pltpu.VMEM((planes, 2, 2, rows, width), bf16),
            pltpu.VMEM((planes, 2, rows, width), bf16),
            pltpu.VMEM((planes, rows, width), bf16),
            pltpu.VMEM((planes, rows, width), bf16),
            pltpu.VMEM((2, 2, rows, width), bf16),
            dma((2,)),
            dma((count - 1,)),
            dma((count - 1,)),
        ]
        + [dma((planes + 1,))] * 16,
        compiler_params=pltpu.CompilerParams(
            collective_id=0, has_side_effects=True, vmem_limit_bytes=60 * 2**20
        ),
    )(resid, norm_gain[None], expert_ids.T, route_weights.T, w_in, w_out)


def local_wide(resid, norm_gain, expert_ids, route_weights, w_in, w_out):
    token_rows, model_width = resid.shape
    top_count = expert_ids.shape[1]
    ep_devices = lax.axis_size("ep")
    capacity = 3 * token_rows * top_count // (2 * ep_devices)
    weight_in = w_in[0]
    weight_out = w_out[0]
    hidden_units = weight_out.shape[0]
    resid_wide = resid.astype(jnp.float32)
    scale = lax.rsqrt(jnp.mean(resid_wide * resid_wide, axis=-1, keepdims=True) + 1e-06)
    normed = (resid_wide * scale * norm_gain).astype(jnp.bfloat16)
    mix_weights = route_weights / jnp.sum(route_weights, axis=-1, keepdims=True)
    flat_ids = expert_ids.reshape(-1)
    onehot = (flat_ids[:, None] == jnp.arange(ep_devices, dtype=jnp.int32)[None, :]).astype(
        jnp.int32
    )
    position = jnp.sum((jnp.cumsum(onehot, axis=0) - onehot) * onehot, axis=1)
    slot_index = flat_ids * capacity + position
    all_normed, all_ids = (
        lax.all_gather(normed, "ep", axis=0, tiled=True),
        lax.all_gather(expert_ids, "ep", axis=0, tiled=True),
    )
    own_expert = lax.axis_index("ep")
    row_hits = (
        jnp.any(all_ids == own_expert, axis=1).astype(jnp.int32).reshape(ep_devices, token_rows)
    )
    placing = jnp.cumsum(row_hits, axis=1) - row_hits
    target = jnp.where(
        row_hits == 1,
        jnp.arange(ep_devices, dtype=jnp.int32)[:, None] * capacity + placing,
        ep_devices * capacity,
    ).reshape(-1)
    received = (
        jnp.zeros((ep_devices * capacity, model_width), jnp.bfloat16)
        .at[target]
        .set(all_normed, mode="drop")
    )
    block_rows = received.reshape(ep_devices, capacity, model_width)
    rows_flat = block_rows.reshape(-1, model_width)
    projected = jnp.dot(rows_flat, weight_in, preferred_element_type=jnp.float32)
    activated = (jax.nn.silu(projected[:, :hidden_units]) * projected[:, hidden_units:]).astype(
        jnp.bfloat16
    )
    produced = jnp.dot(activated, weight_out, preferred_element_type=jnp.float32).astype(
        jnp.bfloat16
    )
    outputs = produced.reshape(block_rows.shape)
    returned = lax.all_to_all(outputs, "ep", split_axis=0, concat_axis=0, tiled=True).reshape(
        -1, model_width
    )
    picked = returned[slot_index].reshape(token_rows, top_count, model_width).astype(jnp.float32)
    mixed = jnp.sum(mix_weights[:, :, None] * picked, axis=1)
    return (resid_wide + mixed).astype(jnp.bfloat16)


def solution(mesh):
    in_specs = (
        P(("groups", "ep"), None),
        P(),
        P(("groups", "ep"), None),
        P(("groups", "ep"), None),
        P("ep", None, None),
        P("ep", None, None),
    )
    out_specs = P(("groups", "ep"), None)
    return jax.shard_map(local, mesh=mesh, in_specs=in_specs, out_specs=out_specs, check_vma=False)
```

```python
import functools

import jax
import jax.numpy as jnp
from jax import lax
from jax.experimental import pallas as pl
from jax.experimental.pallas import tpu as pltpu
from jax.sharding import PartitionSpec as P


PLANE = 4
PARTS = 2
LAG = 2
MESH = pl.DeviceIdType.MESH


def flip(index, bits):
    bit = 1
    while bit <= bits:
        if bits & bit:
            index = index + bit - 2 * bit * ((index // bit) % 2)
        bit *= 2
    return index


def moe_kernel(
    count, resid_ref, gain_ref, ids_ref, route_ref, win_hbm, wout_hbm, o_ref,
    gathered, table_ref, weights, weight_cols, win, wout, hidden, partial, from_core, from_y,
    from_z, from_near,
    load_sem, table_send, table_recv, z_send, z_recv, y_send, y_recv, core_send, core_recv,
    fwd_send, fwd_recv, rc_send, rc_recv, ry_send, ry_recv, rz_send, rz_recv, rn_send, rn_recv,
):
    rows, width = resid_ref.shape
    units = wout.shape[0]
    planes = count // PLANE
    part = rows // PARTS
    me = lax.axis_index("ep")
    z, q = me // PLANE, me % PLANE
    y, c = q // 2, q % 2
    core_mate = z * PLANE + flip(q, 1)
    y_mate = z * PLANE + flip(q, 2)

    def remote(src, dst, send, recv, target):
        return pltpu.make_async_remote_copy(
            src_ref=src, dst_ref=dst, send_sem=send, recv_sem=recv,
            device_id={"ep": target}, device_id_type=MESH,
        )

    load_in = pltpu.make_async_copy(win_hbm.at[0], win, load_sem.at[0])
    load_out = pltpu.make_async_copy(wout_hbm.at[0], wout, load_sem.at[1])
    load_in.start()
    load_out.start()

    barrier = pltpu.get_barrier_semaphore()
    for k in range(1, count):
        pl.semaphore_signal(
            barrier, inc=1, device_id={"ep": lax.rem(me + k, count)}, device_id_type=MESH
        )

    step = 16

    for h in range(PARTS):

        @pl.loop(0, part // step)
        def _(i, h=h):
            at = pl.ds(pl.multiple_of(i * step, step), step)
            wide = resid_ref[pl.ds(pl.multiple_of(h * part + i * step, step), step), :].astype(
                jnp.float32
            )
            scale = lax.rsqrt(jnp.mean(wide * wide, axis=-1, keepdims=True) + 1e-06)
            gathered[z * PARTS + h, q, at, :] = (wide * scale * gain_ref[...]).astype(jnp.bfloat16)

    mix = route_ref[...] / jnp.sum(route_ref[...], axis=0, keepdims=True)
    for e in range(count):
        table_ref[e] = jnp.sum(jnp.where(ids_ref[...] == e, mix, 0.0), axis=0, keepdims=True)
    weights[me] = jnp.sum(jnp.where(ids_ref[...] == me, mix, 0.0), axis=0, keepdims=True)
    pl.semaphore_wait(barrier, count - 1)

    started = []

    def begin(copy):
        copy.start()
        started.append(copy)
        return copy

    low, high = z, planes - 1 - z
    near = jnp.minimum(low, high)
    side = jnp.where(low < high, -1, 1)

    def visit(k):
        if k == 0:
            return z
        paired = (side if k % 2 else -side) * ((k + 1) // 2)
        return z + jnp.where(k <= 2 * near, paired, -side * (k - near))

    plane_of = [visit(k) for k in range(planes)]
    near_planes = [False, True, near >= 1] + [False] * planes
    units_all = planes * PARTS
    is_near = [near_planes[s // PARTS] for s in range(units_all)]
    piece_of = [plane_of[s // PARTS] * PARTS + s % PARTS for s in range(units_all)]

    def when(condition, run):
        if condition is True:
            run()
        elif condition is not False:
            pl.when(condition)(run)

    def negate(condition):
        return not condition if isinstance(condition, bool) else jnp.logical_not(condition)

    to_y, to_core, to_fwd = {}, {}, {}
    red_core, red_y, red_z = {}, {}, {}
    guarded = []

    def begin_if(condition, copy):
        @pl.when(condition)
        def _():
            copy.start()

        guarded.append((condition, copy))

    def spread(s):
        src = dst = gathered.at[piece_of[s], q]
        to_y[s] = begin(remote(src, dst, y_send.at[s], y_recv.at[s], y_mate))
        to_core[s] = begin(remote(src, dst, core_send.at[s], core_recv.at[s], core_mate))

    def forward(s):
        to_y[s].wait_recv()
        block = gathered.at[piece_of[s], flip(q, 2)]
        to_fwd[s] = begin(remote(block, block, fwd_send.at[s], fwd_recv.at[s], core_mate))

    def z_copy(p, src, send, target_plane):
        return remote(
            src, gathered.at[p, q], z_send.at[send], z_recv.at[p], target_plane * PLANE + q
        )

    for s in range(PARTS):
        p = piece_of[s]
        spread(s)
        begin_if(z > 0, z_copy(p, gathered.at[p, q], s, jnp.maximum(z - 1, 0)))
        begin_if(
            z < planes - 1,
            z_copy(p, gathered.at[p, q], units_all + s, jnp.minimum(z + 1, planes - 1)),
        )
    tables = []
    for k in range(1, count):
        target = lax.rem(me + k, count)
        tables.append(
            begin(
                remote(
                    table_ref.at[target], weights.at[me],
                    table_send.at[k - 1], table_recv.at[k - 1], target,
                )
            )
        )
    for slot, there in ((0, z > 0), (1, z < planes - 1)):

        @pl.when(jnp.logical_not(there))
        def _(slot=slot):
            for h in range(PARTS):
                from_near[slot * PARTS + h] = jnp.zeros(from_near.shape[1:], jnp.bfloat16)

    if planes > 2:

        @pl.when(near_planes[2])
        def _():
            for h in range(PARTS):
                from_z[plane_of[2] * PARTS + h] = jnp.zeros(from_z.shape[1:], jnp.bfloat16)

    def arrive(s):
        if s >= units_all:
            return
        p, plane = piece_of[s], plane_of[s // PARTS]
        block = gathered.at[p, q]
        z_copy(p, block, s, plane).wait_recv()
        onward = jnp.where(plane < z, z + 1, z - 1)
        inside = jnp.logical_and(onward >= 0, onward < planes)
        begin_if(inside, z_copy(p, block, s, jnp.clip(onward, 0, planes - 1)))
        spread(s)

    tile_in = 256 if units % 256 == 0 else units
    tile_out = 512 if width % 512 == 0 else width

    def experts(s):
        plane, h = plane_of[s // PARTS], s % PARTS
        eye = lax.broadcasted_iota(jnp.int32, (rows, rows), 0) == lax.broadcasted_iota(
            jnp.int32, (rows, rows), 1
        )
        for k in range(PLANE):
            lane = jnp.broadcast_to(weights[plane * PLANE + k], (rows, rows))
            column = jnp.sum(jnp.where(eye, lane, 0.0), axis=1, keepdims=True)
            weight_cols[pl.ds(k * part, part), :] = jnp.broadcast_to(
                column[h * part : (h + 1) * part], (part, 128)
            )

        @pl.loop(0, units // tile_in)
        def _(j):
            gate_at = pl.multiple_of(j * tile_in, 128)
            up_at = pl.multiple_of(units + j * tile_in, 128)
            block = gathered[piece_of[s]].reshape(PLANE * part, width)
            gate = jnp.dot(
                block, win[:, pl.ds(gate_at, tile_in)], preferred_element_type=jnp.float32
            )
            up = jnp.dot(block, win[:, pl.ds(up_at, tile_in)], preferred_element_type=jnp.float32)
            act = gate / (1.0 + jnp.exp(-gate)) * up
            hidden[:, pl.ds(gate_at, tile_in)] = act.astype(jnp.bfloat16)

        @pl.loop(0, width // tile_out)
        def _(j):
            at = pl.multiple_of(j * tile_out, 128)
            made = jnp.dot(
                hidden[...], wout[:, pl.ds(at, tile_out)], preferred_element_type=jnp.float32
            )
            made = made.astype(jnp.bfloat16).astype(jnp.float32)
            for k in range(PLANE):
                cols = weight_cols[pl.ds(k * part, part), :]
                pieces = [
                    made[k * part : (k + 1) * part, i * 128 : (i + 1) * 128] * cols
                    for i in range(tile_out // 128)
                ]
                partial[s, k % 2, k // 2, :, pl.ds(at, tile_out)] = jnp.concatenate(
                    pieces, axis=1
                ).astype(jnp.bfloat16)

    def reduce_core(s):
        red_core[s] = begin(
            remote(
                partial.at[s, flip(c, 1)], from_core.at[s], rc_send.at[s], rc_recv.at[s], core_mate
            )
        )

    def y_copy(s):
        return remote(
            partial.at[s, c, flip(y, 1)], from_y.at[s], ry_send.at[s], ry_recv.at[s], y_mate
        )

    def far_copy(s, source):
        return remote(
            partial.at[s, c, y], from_z.at[source], rz_send.at[s], rz_recv.at[source],
            plane_of[s // PARTS] * PLANE + q,
        )

    def near_copy(s, slot):
        return remote(
            partial.at[s, c], from_near.at[slot], rn_send.at[s], rn_recv.at[slot],
            plane_of[s // PARTS] * PLANE + q,
        )

    def reduce_y(s):
        red_core[s].wait_recv()
        if s < PARTS:
            for slot, there in ((0, z > 0), (1, z < planes - 1)):

                @pl.when(there)
                def _(slot=slot):
                    near_copy(s, slot * PARTS + s).wait_recv()

        @pl.loop(0, part // step)
        def _(i):
            at = pl.ds(pl.multiple_of(i * step, step), step)
            for k in range(2):
                total = partial[s, c, k, at, :].astype(jnp.float32) + from_core[
                    s, k, at, :
                ].astype(jnp.float32)
                if s < PARTS:
                    for slot in range(2):
                        total = total + from_near[slot * PARTS + s, k, at, :].astype(jnp.float32)
                partial[s, c, k, at, :] = total.astype(jnp.bfloat16)

        side_slot = jnp.where(plane_of[s // PARTS] > z, 0, PARTS)
        when(is_near[s], lambda: near_copy(s, side_slot + s % PARTS).start())
        when(negate(is_near[s]), lambda: y_copy(s).start())

    def reduce_z(s):
        def run():
            y_copy(s).wait_recv()

            @pl.loop(0, part // step)
            def _(i):
                at = pl.ds(pl.multiple_of(i * step, step), step)
                total = partial[s, c, y, at, :].astype(jnp.float32) + from_y[s, at, :].astype(
                    jnp.float32
                )
                partial[s, c, y, at, :] = total.astype(jnp.bfloat16)

            far_copy(s, z * PARTS + s % PARTS).start()

        when(negate(is_near[s]), run)

    arrive(PARTS)
    forward(0)
    load_in.wait()
    load_out.wait()
    for copy in tables:
        copy.wait_recv()
    arrive(PARTS + 1)
    for s in range(units_all):
        to_core[s].wait_recv()
        to_fwd[s].wait_recv()
        experts(s)
        reduce_core(s)
        arrive(s + PARTS + 2)
        if s + 1 < units_all:
            forward(s + 1)
        if s >= PARTS:
            reduce_y(s)
        if s >= 2 * PARTS + LAG:
            reduce_z(s - LAG)
    for s in range(max(units_all - LAG, 2 * PARTS), units_all):
        reduce_z(s)
    for s in range(PARTS):
        reduce_y(s)
    for s in range(PARTS):
        y_copy(s).wait_recv()
    for s in range(2 * PARTS, units_all):
        when(negate(is_near[s]), lambda s=s: far_copy(s, piece_of[s]).wait_recv())

    for h in range(PARTS):

        @pl.loop(0, part // step)
        def _(i, h=h):
            at = pl.ds(pl.multiple_of(i * step, step), step)
            out_at = pl.ds(pl.multiple_of(h * part + i * step, step), step)
            total = partial[h, c, y, at, :].astype(jnp.float32)
            total = total + from_y[h, at, :].astype(jnp.float32)
            for s in range(2, planes):
                total = total + from_z[plane_of[s] * PARTS + h, at, :].astype(jnp.float32)
            o_ref[out_at, :] = (resid_ref[out_at, :].astype(jnp.float32) + total).astype(
                jnp.bfloat16
            )

    for copy in started:
        copy.wait_send()
    for condition, copy in guarded:

        @pl.when(condition)
        def _(copy=copy):
            copy.wait_send()

    for s in range(PARTS):
        y_copy(s).wait_send()
    for s in range(PARTS, units_all):
        when(is_near[s], lambda s=s: near_copy(s, 0).wait_send())

        def sent(s=s):
            y_copy(s).wait_send()
            far_copy(s, z * PARTS + s % PARTS).wait_send()

        when(negate(is_near[s]), sent)


def vmem_bytes(count, rows, width, units):
    block = 2 * rows * width
    return (
        block * (4 * 2 * (count // PLANE) + 8) + 2 * 3 * units * width
        + 2 * PLANE * rows * units + 8 * count * rows * 4
    )


def local(resid, norm_gain, expert_ids, route_weights, w_in, w_out):
    rows, width = resid.shape
    units = w_out.shape[1]
    count = lax.axis_size("ep")
    planes = count // PLANE
    fits = vmem_bytes(count, rows, width, units) <= 44 * 2**20
    if count % PLANE or planes < 2 or planes & (planes - 1) or rows != 128 or not fits:
        return local_wide(resid, norm_gain, expert_ids, route_weights, w_in, w_out)
    part, pieces = rows // PARTS, planes * PARTS
    vmem = pl.BlockSpec(memory_space=pltpu.VMEM)
    hbm = pl.BlockSpec(memory_space=pl.ANY)
    bf16 = jnp.bfloat16
    dma = pltpu.SemaphoreType.DMA
    return pl.pallas_call(
        functools.partial(moe_kernel, count),
        out_shape=jax.ShapeDtypeStruct((rows, width), bf16),
        in_specs=[vmem, vmem, vmem, vmem, hbm, hbm],
        out_specs=vmem,
        scratch_shapes=[
            pltpu.VMEM((pieces, PLANE, part, width), bf16),
            pltpu.VMEM((count, 1, rows), jnp.float32),
            pltpu.VMEM((count, 1, rows), jnp.float32),
            pltpu.VMEM((PLANE * part, 128), jnp.float32),
            pltpu.VMEM((width, 2 * units), bf16),
            pltpu.VMEM((units, width), bf16),
            pltpu.VMEM((PLANE * part, units), bf16),
            pltpu.VMEM((pieces, 2, 2, part, width), bf16),
            pltpu.VMEM((pieces, 2, part, width), bf16),
            pltpu.VMEM((pieces, part, width), bf16),
            pltpu.VMEM((pieces, part, width), bf16),
            pltpu.VMEM((2 * PARTS, 2, part, width), bf16),
            dma((2,)),
            dma((count - 1,)),
            dma((count - 1,)),
        ]
        + [dma((pieces + PARTS,))] * 16,
        compiler_params=pltpu.CompilerParams(
            collective_id=0, has_side_effects=True, vmem_limit_bytes=60 * 2**20
        ),
    )(resid, norm_gain[None], expert_ids.T, route_weights.T, w_in, w_out)


def local_wide(resid, norm_gain, expert_ids, route_weights, w_in, w_out):
    token_rows, model_width = resid.shape
    top_count = expert_ids.shape[1]
    ep_devices = lax.axis_size("ep")
    capacity = 3 * token_rows * top_count // (2 * ep_devices)
    weight_in = w_in[0]
    weight_out = w_out[0]
    hidden_units = weight_out.shape[0]
    resid_wide = resid.astype(jnp.float32)
    scale = lax.rsqrt(jnp.mean(resid_wide * resid_wide, axis=-1, keepdims=True) + 1e-06)
    normed = (resid_wide * scale * norm_gain).astype(jnp.bfloat16)
    mix_weights = route_weights / jnp.sum(route_weights, axis=-1, keepdims=True)
    flat_ids = expert_ids.reshape(-1)
    onehot = (flat_ids[:, None] == jnp.arange(ep_devices, dtype=jnp.int32)[None, :]).astype(
        jnp.int32
    )
    position = jnp.sum((jnp.cumsum(onehot, axis=0) - onehot) * onehot, axis=1)
    slot_index = flat_ids * capacity + position
    all_normed, all_ids = (
        lax.all_gather(normed, "ep", axis=0, tiled=True),
        lax.all_gather(expert_ids, "ep", axis=0, tiled=True),
    )
    own_expert = lax.axis_index("ep")
    row_hits = (
        jnp.any(all_ids == own_expert, axis=1).astype(jnp.int32).reshape(ep_devices, token_rows)
    )
    placing = jnp.cumsum(row_hits, axis=1) - row_hits
    target = jnp.where(
        row_hits == 1,
        jnp.arange(ep_devices, dtype=jnp.int32)[:, None] * capacity + placing,
        ep_devices * capacity,
    ).reshape(-1)
    received = (
        jnp.zeros((ep_devices * capacity, model_width), jnp.bfloat16)
        .at[target]
        .set(all_normed, mode="drop")
    )
    block_rows = received.reshape(ep_devices, capacity, model_width)
    rows_flat = block_rows.reshape(-1, model_width)
    projected = jnp.dot(rows_flat, weight_in, preferred_element_type=jnp.float32)
    activated = (jax.nn.silu(projected[:, :hidden_units]) * projected[:, hidden_units:]).astype(
        jnp.bfloat16
    )
    produced = jnp.dot(activated, weight_out, preferred_element_type=jnp.float32).astype(
        jnp.bfloat16
    )
    outputs = produced.reshape(block_rows.shape)
    returned = lax.all_to_all(outputs, "ep", split_axis=0, concat_axis=0, tiled=True).reshape(
        -1, model_width
    )
    picked = returned[slot_index].reshape(token_rows, top_count, model_width).astype(jnp.float32)
    mixed = jnp.sum(mix_weights[:, :, None] * picked, axis=1)
    return (resid_wide + mixed).astype(jnp.bfloat16)


def solution(mesh):
    in_specs = (
        P(("groups", "ep"), None),
        P(),
        P(("groups", "ep"), None),
        P(("groups", "ep"), None),
        P("ep", None, None),
        P("ep", None, None),
    )
    out_specs = P(("groups", "ep"), None)
    return jax.shard_map(local, mesh=mesh, in_specs=in_specs, out_specs=out_specs, check_vma=False)
```
